256 devices in a mesh: dp: 4 (over x), expert: 64 (over y, z, core).
Axes of the slice: x: 4, y: 4, z: 8, core: 2. Of those that a mesh axis runs over, the one named last changes fastest.
Arguments:
- tokens: bfloat16 [4096, 4096], P(('dp', 'expert')), may hold values from -6 to 6
- out_grad: bfloat16 [4096, 4096], P(('dp', 'expert')), may hold values from -6 to 6
- routes: int32 [4096, 8], P(('dp', 'expert')), may hold values from 0 to 63, all different within a row; in each aligned block of 16 rows (0 to 15, 16 to 31, ...) at most 4 rows name the same one
- router_weights: float32 [4096, 8], P(('dp', 'expert')), may hold values from 0.05 to 0.5
- w_gate: bfloat16 [64, 768, 4096], P('expert', 'dp'), may hold values from -0.09375 to 0.09375
- w_up: bfloat16 [64, 768, 4096], P('expert', 'dp'), may hold values from -0.09375 to 0.09375
- w_down: bfloat16 [64, 768, 4096], P('expert', 'dp'), may hold values from -0.21875 to 0.21875
Outputs:
- grad_tokens: bfloat16 [4096, 4096], P(('dp', 'expert'))
- grad_gate: bfloat16 [64, 768, 4096], P('expert', 'dp')
- grad_up: bfloat16 [64, 768, 4096], P('expert', 'dp')
- grad_down: bfloat16 [64, 768, 4096], P('expert', 'dp')
The draws below stay inside these ranges and needn't reach their ends.
Inputs may be any that keep to these rules, and one draw needn't show every extreme that they name: `routes`: each token names 8 different experts; among the tokens of one device no expert is named more than 4 times, a bound that some block reaches.
All inputs are finite; a program needn't handle non-finite values.
Results may differ from the reference program's by a relative error of at most 0.015.
Values may be sent and summed in bfloat16 or wider, within the bound.
No kernel may reach another device: no remote copies, remote signals or barrier semaphores. Data moves between devices by JAX's collectives and lax.ppermute only.
A program may use at most 128 MiB of HBM per device.

```python
import math
import jax
import jax.numpy as jnp
import numpy as np
from jax import lax

D = 4096
FF = 768
TOP = 8
TOK_DEV = 16
EXPERTS = 64
CAP = 4
TOKENS = 4096
N_DP = 4


def levels(own_key, extent, split, least, high):
    def one(dim, parts):
        heights = jax.random.uniform(jax.random.fold_in(jax.random.fold_in(own_key, 6), dim), (parts,), jnp.float32, least / len(split), high / len(split))
        return jnp.repeat(jnp.exp(heights), extent[dim] // parts).reshape((-1,) + (1,) * (len(extent) - dim - 1))

    level = one(*split[0])
    for cut in split[1:]:
        level = level * one(*cut)
    return level


def deal_out(own_key, own, number, rows, number_of, top, bound, lean):
    sequence = jax.random.permutation(own_key, number_of)
    packed, common = portions_of(number_of, rows * top, bound, lean, True), portions_of(number_of, rows * top, bound, lean, False)
    places = jnp.arange(number_of)

    def named(tallies, turn):
        used = int((tallies > 0).sum())
        fixed = max(1, used // 4)
        shifted = fixed + (places - fixed + turn * (used - fixed)) % max(1, number_of - fixed)
        return jnp.zeros((number_of,), jnp.int32).at[sequence[jnp.where(places < fixed, places, shifted)]].set(jnp.asarray(tallies, jnp.int32))

    tallies = jnp.where(number % 4 == 0, named(packed, number // 4), named(common, number - number // 4 - 1))
    mixed = jax.random.permutation(jax.random.fold_in(own, 3), number_of)
    donor, receiver = mixed[0:number_of // 2 * 2:2], mixed[1:number_of // 2 * 2:2]
    room = jnp.minimum(tallies[donor] - 1, bound - tallies[receiver]) // 2
    room = jnp.where((donor == sequence[0]) | (receiver == sequence[0]) | (tallies[receiver] == 0), 0, jnp.maximum(room, 0))
    shifted = jax.random.randint(jax.random.fold_in(own, 4), (number_of // 2,), 0, 1 << 20) % (room + 1)
    tallies = tallies.at[donor].add(-shifted).at[receiver].add(shifted)
    items = jnp.searchsorted(jnp.cumsum(tallies), jnp.arange(rows * top), side="right").astype(jnp.int32)
    grid = items.reshape(top, rows).T
    grid = grid[jax.random.permutation(jax.random.fold_in(own, 1), rows)]
    turn = jax.random.randint(jax.random.fold_in(own, 2), (rows, 1), 0, top)
    return jnp.take_along_axis(grid, (jnp.arange(top)[None, :] + turn) % top, axis=1)


def portions_of(number_of, total, limit, slope, full):
    portions = [(1 << 20) // math.isqrt(grade ** slope) + 1 for grade in range(1, number_of + 1)]
    largest = limit if full else min(limit, max(-(-total // number_of), total * portions[0] // sum(portions)))
    least = 1 if total - largest >= number_of - 1 else 0
    given, surplus = [largest] + [least] * (number_of - 1), total - largest - least * (number_of - 1)
    while surplus > 0:
        candidates = [i for i in range(1, number_of) if given[i] < largest] or [i for i in range(1, number_of) if given[i] < limit]
        mass, left = sum([portions[i] for i in candidates]), surplus
        for i in candidates:
            addition = min(limit - given[i], max(1, left * portions[i] // mass), surplus)
            given[i] = given[i] + addition
            surplus = surplus - addition
    return np.array(given)


def noise(own_key, shape, spread, reach, pieces=(), held_as=jnp.bfloat16):
    factor_of = levels(own_key, shape, pieces, -0.22, 0.18) if pieces else 1.0
    array = jax.random.normal(own_key, shape, jnp.float32) * spread * factor_of
    return jnp.minimum(jnp.maximum(array, -reach), reach).astype(held_as)


def setup_inputs(seed: int = 0) -> dict:
    splits = jax.random.split(jax.random.key(seed), 8)
    tokens = noise(splits[0], (TOKENS, D), 1.0, 6.0, ((0, 256),))
    out_grad = noise(splits[1], (TOKENS, D), 1.0, 6.0, ((0, 256),))
    routes_keys = jax.random.split(jax.random.fold_in(splits[2], 1), TOKENS // TOK_DEV)
    routes_turns = jax.random.permutation(jax.random.fold_in(splits[2], 3), TOKENS // TOK_DEV)
    routes = jax.vmap(lambda own, number: deal_out(jax.random.fold_in(splits[2], 2), own, number, TOK_DEV, EXPERTS, TOP, CAP, 2))(routes_keys, routes_turns).reshape((TOKENS, TOP))
    router_weights = jnp.clip(jnp.exp(math.log(0.5) - 2.3025851 * jax.random.uniform(splits[3], (TOKENS, TOP), jnp.float32) ** levels(splits[3], (TOKENS, TOP), ((0, 256),), -0.2, 0.2)), 0.05, 0.5)
    w_gate = noise(splits[4], (EXPERTS, FF, D), D ** -0.5, 0.09375, ((0, 64), (1, 4)))
    w_up = noise(splits[5], (EXPERTS, FF, D), D ** -0.5, 0.09375, ((0, 64), (1, 4)))
    w_down = noise(splits[6], (EXPERTS, FF, D), FF ** -0.5, 0.21875, ((0, 64), (1, 4)))
    return {"tokens": tokens, "out_grad": out_grad, "routes": routes, "router_weights": router_weights, "w_gate": w_gate, "w_up": w_up, "w_down": w_down}


def reference(tokens, out_grad, routes, router_weights, w_gate, w_up, w_down):
    picks = TOKENS * TOP
    tile_rows = 128
    flat = routes.reshape(picks).astype(jnp.int32)
    owner = (jnp.arange(picks, dtype=jnp.int32) // TOP).astype(jnp.int32)
    scaled = (out_grad.astype(jnp.float32)[:, None, :] * router_weights.astype(jnp.float32)[:, :, None]).astype(jnp.bfloat16).reshape(picks, D)
    order = jnp.argsort(flat, stable=True).astype(jnp.int32)
    order = jnp.concatenate([order, jnp.zeros((tile_rows,), jnp.int32)]).astype(jnp.int32)
    counts = jnp.zeros((EXPERTS,), jnp.int32).at[flat].add(1)
    starts = (jnp.cumsum(counts) - counts).astype(jnp.int32)
    block = FF // N_DP

    def one_expert(grad_acc, item):
        expert_no, gate_w, up_w, down_w = item
        count = counts[expert_no]
        start = starts[expert_no]
        tiles = (count + tile_rows - 1) // tile_rows
        gate_blocks = gate_w.astype(jnp.float32).reshape(N_DP, block, D)
        up_blocks = up_w.astype(jnp.float32).reshape(N_DP, block, D)

        def step(turn, carry):
            sum_down, sum_gate, sum_up, acc = carry
            offset = (start + turn * tile_rows).astype(jnp.int32)
            where_from = lax.dynamic_slice_in_dim(order, offset, tile_rows)
            valid = (turn * tile_rows + jnp.arange(tile_rows, dtype=jnp.int32)) < count
            token_no = owner[where_from]
            tile_in = jnp.where(valid[:, None], tokens[token_no], 0).astype(jnp.bfloat16)
            tile_grad = jnp.where(valid[:, None], scaled[where_from], 0).astype(jnp.bfloat16)
            gate = jnp.dot(tile_in, gate_w.T, preferred_element_type=jnp.float32)
            upward = jnp.dot(tile_in, up_w.T, preferred_element_type=jnp.float32)
            back = jnp.dot(tile_grad, down_w.T, preferred_element_type=jnp.float32)
            sigma = jax.nn.sigmoid(gate)
            active = gate * sigma
            hidden = (active * upward).astype(jnp.bfloat16)
            d_gate = (back * upward * sigma * (1.0 + gate * (1.0 - sigma))).astype(jnp.bfloat16)
            d_up = (back * active).astype(jnp.bfloat16)
            sum_down = sum_down + jnp.dot(hidden.T, tile_grad, preferred_element_type=jnp.float32)
            sum_gate = sum_gate + jnp.dot(d_gate.T, tile_in, preferred_element_type=jnp.float32)
            sum_up = sum_up + jnp.dot(d_up.T, tile_in, preferred_element_type=jnp.float32)
            gate_parts = d_gate.astype(jnp.float32).reshape(tile_rows, N_DP, block)
            up_parts = d_up.astype(jnp.float32).reshape(tile_rows, N_DP, block)
            partial_value = jnp.einsum("tkf,kfd->ktd", gate_parts, gate_blocks) + jnp.einsum("tkf,kfd->ktd", up_parts, up_blocks)
            rounded = lax.optimization_barrier(partial_value.astype(jnp.bfloat16))
            row = jnp.sum(rounded.astype(jnp.float32), axis=0).astype(jnp.bfloat16)
            row = lax.optimization_barrier(row).astype(jnp.float32)
            acc = acc.at[token_no].add(jnp.where(valid[:, None], row, jnp.float32(0.0)))
            return sum_down, sum_gate, sum_up, acc

        zeros = jnp.zeros((FF, D), jnp.float32)
        sum_down, sum_gate, sum_up, grad_acc = lax.fori_loop(0, tiles, step, (zeros, zeros, zeros, grad_acc))
        return grad_acc, (sum_gate.astype(jnp.bfloat16), sum_up.astype(jnp.bfloat16), sum_down.astype(jnp.bfloat16))

    start_acc = jnp.zeros((TOKENS, D), jnp.float32)
    items = (jnp.arange(EXPERTS, dtype=jnp.int32), w_gate, w_up, w_down)
    grad_acc, outs = lax.scan(one_expert, start_acc, items)
    grad_gate, grad_up, grad_down = outs
    return grad_acc.astype(jnp.bfloat16), grad_gate, grad_up, grad_down
```

```python
import functools

import jax
import jax.numpy as jnp
from jax import lax
from jax.experimental import pallas as pl
from jax.experimental.pallas import tpu as pltpu
from jax.sharding import Mesh
from jax.sharding import PartitionSpec as P

BF16 = jnp.bfloat16
F32 = jnp.float32
ALL = ("x", "y", "z", "c")


def shift(value, axis, by):
    size = lax.axis_size(axis)
    return lax.ppermute(value, axis, [(i, (i + by) % size) for i in range(size)])


def add(first, *others):
    total = first.astype(F32)
    for other in others:
        total = total + other.astype(F32)
    return total.astype(BF16)


def ring_sum4(own, near, opposite, back, axis):
    half = opposite.shape[0] // 2
    up = shift(opposite[:half], axis, 1)
    down = shift(opposite[half:], axis, -1)
    near = jnp.concatenate([add(near[:half], up), near[half:]], axis=0)
    back = jnp.concatenate([back[:half], add(back[half:], down)], axis=0)
    return add(own, shift(near, axis, 1), shift(back, axis, -1))


def token_kernel(ids, t_ref, g_ref, m_ref, wgu_ref, wd_ref, p_ref, dgu_ref, h_ref):
    rows = t_ref.shape[0] * t_ref.shape[1] * t_ref.shape[2] * t_ref.shape[5]
    width = t_ref.shape[6]
    hid = wd_ref.shape[0]
    t = t_ref[...].reshape(rows, width)
    g = g_ref[...].reshape(rows, width)
    meta = m_ref[...].reshape(rows, m_ref.shape[-1])
    top = meta.shape[1] // 2
    routes, probs = meta[:, :top], meta[:, top:]
    zero = jnp.float32(0)
    mine = jnp.sum(jnp.where(routes == ids[3].astype(F32), probs, zero), axis=1, keepdims=True)
    other = jnp.sum(jnp.where(routes == ids[4].astype(F32), probs, zero), axis=1, keepdims=True)
    column = lax.broadcasted_iota(jnp.int32, (rows, hid), 1)
    weight = jnp.where(column < hid // 2, mine, other)
    wide = (((1,), (1,)), ((), ()))
    gate_up = lax.dot_general(t, wgu_ref[...], wide, preferred_element_type=F32)
    back = lax.dot_general(g, wd_ref[...], wide, preferred_element_type=F32) * weight
    gate, upward = gate_up[:, :hid], gate_up[:, hid:]
    sigma = jax.nn.sigmoid(gate)
    active = gate * sigma
    hidden = active * upward * weight
    d_gate = back * upward * sigma * (1.0 + gate * (1.0 - sigma))
    d_up = back * active
    both = jnp.concatenate([d_gate, d_up], axis=1)
    h_ref[...] = hidden.T.astype(BF16).reshape(h_ref.shape)
    dgu_ref[...] = both.T.astype(BF16).reshape(dgu_ref.shape)
    partial = jnp.dot(both.astype(BF16), wgu_ref[...], preferred_element_type=F32)
    p_ref[...] = partial.astype(BF16).reshape(p_ref.shape)


def token_call(ids, rows, meta, wgu, wd, part):
    nx, ny, nz, _, _, per, width = rows.shape
    half = per // 2
    hid = wd.shape[0]
    if part == 0:
        steps, block = nx, (1, ny, nz)
        place = lambda i, ids: (lax.rem(ids[0] + i, nx), 0, 0)
        absolute = lambda i, ids: lax.rem(ids[0] + i, nx)
    else:
        steps, block = ny, (nx, 1, nz)
        place = lambda i, ids: (0, lax.rem(ids[1] + i, ny), 0)
        absolute = lambda i, ids: lax.rem(ids[1] + i, ny)
    count = block[0] * block[1] * block[2] * half
    across = block[0] * block[1]
    return pl.pallas_call(
        token_kernel,
        grid_spec=pltpu.PrefetchScalarGridSpec(
            num_scalar_prefetch=1,
            grid=(steps,),
            in_specs=[
                pl.BlockSpec((*block, 1, 1, half, width), lambda i, ids: (*place(i, ids), ids[2], 0, part, 0)),
                pl.BlockSpec((*block, 1, 1, half, width), lambda i, ids: (*place(i, ids), ids[2], 1, part, 0)),
                pl.BlockSpec((*block, 1, half, meta.shape[-1]), lambda i, ids: (*place(i, ids), ids[2], part, 0)),
                pl.BlockSpec(wgu.shape, lambda i, ids: (0, 0), pipeline_mode=pl.Buffered(1)),
                pl.BlockSpec(wd.shape, lambda i, ids: (0, 0), pipeline_mode=pl.Buffered(1)),
            ],
            out_specs=[
                pl.BlockSpec((1, across, nz, half, width), lambda i, ids: (i, 0, 0, 0, 0)),
                pl.BlockSpec((1, 2 * hid, count), lambda i, ids: (absolute(i, ids), 0, 0)),
                pl.BlockSpec((1, hid, count), lambda i, ids: (absolute(i, ids), 0, 0)),
            ],
        ),
        out_shape=[
            jax.ShapeDtypeStruct((steps, across, nz, half, width), BF16),
            jax.ShapeDtypeStruct((steps, 2 * hid, count), BF16),
            jax.ShapeDtypeStruct((steps, hid, count), BF16),
        ],
        compiler_params=pltpu.CompilerParams(vmem_limit_bytes=56 << 20),
        name=f"tokens{part}",
    )(ids, rows, rows, meta, wgu, wd)


def weight_kernel(ids, t_ref, g_ref, dgu0_ref, dgu1_ref, h0_ref, h1_ref, mine_ref, other_ref):
    nx, ny, nz, _, _, per, tile = t_ref.shape
    half = per // 2
    unit = h0_ref.shape[1] // 2

    def outer(first, second, ref):
        total = None
        for i in range(nx):
            right = ref[i, :, :, 0, 0, :half, :].reshape(-1, tile)
            term = jnp.dot(first[i], right, preferred_element_type=F32)
            total = term if total is None else total + term
        for i in range(ny):
            right = ref[:, i, :, 0, 0, half:, :].reshape(-1, tile)
            total = total + jnp.dot(second[i], right, preferred_element_type=F32)
        return total

    gu = outer(dgu0_ref, dgu1_ref, t_ref)
    down = outer(h0_ref, h1_ref, g_ref)
    mine_ref[0] = gu[:unit]
    mine_ref[1] = gu[2 * unit : 3 * unit]
    mine_ref[2] = down[:unit]
    other_ref[0] = gu[unit : 2 * unit].astype(BF16)
    other_ref[1] = gu[3 * unit :].astype(BF16)
    other_ref[2] = down[unit:].astype(BF16)


def weight_call(ids, rows, dgu0, dgu1, h0, h1):
    nx, ny, nz, _, _, per, width = rows.shape
    unit = h0.shape[1] // 2
    tile = 512
    whole = lambda a: pl.BlockSpec(a.shape, lambda j, ids: (0, 0, 0), pipeline_mode=pl.Buffered(1))
    return pl.pallas_call(
        weight_kernel,
        grid_spec=pltpu.PrefetchScalarGridSpec(
            num_scalar_prefetch=1,
            grid=(width // tile,),
            in_specs=[
                pl.BlockSpec((nx, ny, nz, 1, 1, per, tile), lambda j, ids: (0, 0, 0, ids[2], 0, 0, j)),
                pl.BlockSpec((nx, ny, nz, 1, 1, per, tile), lambda j, ids: (0, 0, 0, ids[2], 1, 0, j)),
                whole(dgu0),
                whole(dgu1),
                whole(h0),
                whole(h1),
            ],
            out_specs=[
                pl.BlockSpec((3, unit, tile), lambda j, ids: (0, 0, j)),
                pl.BlockSpec((3, unit, tile), lambda j, ids: (0, 0, j)),
            ],
        ),
        out_shape=[
            jax.ShapeDtypeStruct((3, unit, width), F32),
            jax.ShapeDtypeStruct((3, unit, width), BF16),
        ],
        compiler_params=pltpu.CompilerParams(vmem_limit_bytes=56 << 20),
        name="weights",
    )(ids, rows, rows, dgu0, dgu1, h0, h1)


def on_device(tokens, out_grad, routes, router_weights, w_gate, w_up, w_down):
    nx, ny, nz, nc = (lax.axis_size(a) for a in ALL)
    ix, iy, iz, ic = (lax.axis_index(a) for a in ALL)
    per, width = tokens.shape
    top = routes.shape[1]
    expert = (iy * nz + iz) * nc + ic
    ids = jnp.stack([ix, iy, ic, expert, expert + 1 - 2 * ic]).astype(jnp.int32)

    rows = lax.all_gather(jnp.concatenate([tokens, out_grad], axis=0), ALL, axis=0, tiled=True)
    rows = rows.reshape(nx, ny, nz, nc, 2, per, width)
    meta = jnp.concatenate([routes.astype(F32), router_weights], axis=1)
    meta = lax.all_gather(meta, ALL, axis=0, tiled=True).reshape(nx, ny, nz, nc, per, 2 * top)

    packed = jnp.concatenate([w_gate, w_up, w_down], axis=0)
    swapped = shift(packed, "c", 1)
    wgu = jnp.concatenate([w_gate[0], swapped[0], w_up[0], swapped[1]], axis=0)
    wd = jnp.concatenate([w_down[0], swapped[2]], axis=0)

    p0, dgu0, h0 = token_call(ids, rows, meta, wgu, wd, 0)
    p1, dgu1, h1 = token_call(ids, rows, meta, wgu, wd, 1)
    mine, other = weight_call(ids, rows, dgu0, dgu1, h0, h1)

    q0 = ring_sum4(p0[0], p0[1], p0[2], p0[3], "x")
    q1 = ring_sum4(p1[0], p1[1], p1[2], p1[3], "y")
    pick = lambda q, at, size: lax.dynamic_index_in_dim(q, lax.rem(at, size), 0, keepdims=False)
    r0 = ring_sum4(*(pick(q0, iy + k, ny) for k in range(4)), "y")
    r1 = ring_sum4(*(pick(q1, ix + k, nx) for k in range(4)), "x")
    both = jnp.concatenate([r0, r1], axis=1).reshape(nz * per, width)
    grad_tokens = lax.psum_scatter(both, "z", scatter_dimension=0, tiled=True)

    grads = (mine + shift(other, "c", 1).astype(F32)).astype(BF16)
    return grad_tokens, grads[0:1], grads[1:2], grads[2:3]


def solution(mesh):
    fine = Mesh(mesh.devices.reshape(4, 4, 8, 2), ALL)
    row = P(ALL, None)
    weight = P(("y", "z", "c"), "x", None)
    return jax.shard_map(
        on_device,
        mesh=fine,
        in_specs=(row, row, row, row, weight, weight, weight),
        out_specs=(row, weight, weight, weight),
        check_vma=False,
    )
```

```python
import functools

import jax
import jax.numpy as jnp
from jax import lax
from jax.experimental import pallas as pl
from jax.experimental.pallas import tpu as pltpu
from jax.sharding import Mesh
from jax.sharding import PartitionSpec as P

BF16 = jnp.bfloat16
F32 = jnp.float32
ALL = ("x", "y", "z", "c")


def shift(value, axis, by):
    size = lax.axis_size(axis)
    return lax.ppermute(value, axis, [(i, (i + by) % size) for i in range(size)])


def add(first, *others):
    total = first.astype(F32)
    for other in others:
        total = total + other.astype(F32)
    return total.astype(BF16)


def ring_ends(up, down, axis):
    return shift(up, axis, 1), shift(down, axis, -1)


def ring_ends4(opposite, axis):
    half = opposite.shape[0] // 2
    return ring_ends(opposite[:half], opposite[half:], axis)


def ring_middle4(near, back, ends):
    half = ends[0].shape[0]
    near = jnp.concatenate([add(near[:half], ends[0]), near[half:]], axis=0)
    back = jnp.concatenate([back[:half], add(back[half:], ends[1])], axis=0)
    return near, back


def ring_sum4(own, near, opposite, back, axis):
    near, back = ring_middle4(near, back, ring_ends4(opposite, axis))
    return add(own, *ring_ends(near, back, axis))


def ring_gather4(first, first_axis, second, second_axis, beside=()):
    near0, back0 = shift(first, first_axis, -1), shift(first, first_axis, 1)
    near1, back1 = shift(second, second_axis, -1), shift(second, second_axis, 1)
    near0, back0, near1, back1, beside = lax.optimization_barrier((near0, back0, near1, back1, beside))
    far = lambda near, back, axis, half: (shift(near[:half], axis, -1), shift(back[half:], axis, 1))
    far0 = far(near0, back0, first_axis, first.shape[0] // 2)
    far1 = far(near1, back1, second_axis, second.shape[0] // 2)
    return (first, near0, *far0, back0), (second, near1, *far1, back1), beside


def joined4(parts):
    own, near, first, second, back = parts
    return jnp.stack([own, near, jnp.concatenate([first, second], axis=0), back])


def ring_gather_z(left, right, axis):
    size, cut = lax.axis_size(axis), left.shape[1]
    own = jnp.concatenate([left, right], axis=1)
    up, down = [own], [own]
    for _ in range(size // 2 - 1):
        up.append(shift(up[-1], axis, -1))
        down.append(shift(down[-1], axis, 1))
    lefts = [b[:, :cut] for b in up] + [shift(up[-1][:, :cut], axis, -1)] + [b[:, :cut] for b in down[:0:-1]]
    rights = [b[:, cut:] for b in up] + [shift(down[-1][:, cut:], axis, 1)] + [b[:, cut:] for b in down[:0:-1]]
    return jnp.stack(lefts), jnp.stack(rights)


def expert_terms(ids, t, g, meta, wgu_ref, wd_ref, p_ref, dgu_ref, h_ref):
    rows, lanes = meta.shape
    hid = wd_ref.shape[0]
    lane = lax.rem(lax.broadcasted_iota(jnp.int32, (rows, lanes), 1), lanes // 2)
    values = meta.astype(F32)
    zero = jnp.float32(0)
    mine = jnp.sum(jnp.where(lane == ids[3], values, zero), axis=1, keepdims=True)
    other = jnp.sum(jnp.where(lane == ids[4], values, zero), axis=1, keepdims=True)
    column = lax.broadcasted_iota(jnp.int32, (rows, hid), 1)
    weight = jnp.where(column < hid // 2, mine, other)
    wide = (((1,), (1,)), ((), ()))
    gate_up = lax.dot_general(t, wgu_ref[...], wide, preferred_element_type=F32)
    back = lax.dot_general(g, wd_ref[...], wide, preferred_element_type=F32) * weight
    gate, upward = gate_up[:, :hid], gate_up[:, hid:]
    sigma = jax.nn.sigmoid(gate)
    active = gate * sigma
    hidden = (active * upward * weight).astype(BF16)
    d_gate = (back * upward * sigma * (1.0 + gate * (1.0 - sigma))).astype(BF16)
    d_up = (back * active).astype(BF16)
    both = jnp.concatenate([d_gate, d_up], axis=1)
    h_ref[...] = hidden.T.reshape(h_ref.shape)
    dgu_ref[...] = both.T.reshape(dgu_ref.shape)
    partial = jnp.dot(both, wgu_ref[...], preferred_element_type=F32)
    p_ref[...] = partial.astype(BF16).reshape(p_ref.shape)


def first_kernel(ids, t_ref, g_ref, m_ref, wgu_ref, wd_ref, p_ref, dgu_ref, h_ref):
    rows = t_ref.shape[1] * t_ref.shape[2] * t_ref.shape[5]
    flat = lambda ref: ref[...].reshape(rows, ref.shape[-1])
    expert_terms(ids, flat(t_ref), flat(g_ref), flat(m_ref), wgu_ref, wd_ref, p_ref, dgu_ref, h_ref)


def first_call(ids, rows, wgu, wd, lanes):
    nx, ny, nz, _, _, half, _ = rows.shape
    width = wgu.shape[1]
    hid = wd.shape[0]
    count = ny * nz * half
    at = lambda i, ids: lax.rem(ids[0] + i, nx)
    return pl.pallas_call(
        first_kernel,
        grid_spec=pltpu.PrefetchScalarGridSpec(
            num_scalar_prefetch=1,
            grid=(nx,),
            in_specs=[
                pl.BlockSpec((1, ny, nz, 1, 1, half, width), lambda i, ids: (at(i, ids), 0, 0, ids[2], 0, 0, 0)),
                pl.BlockSpec((1, ny, nz, 1, 1, half, width), lambda i, ids: (at(i, ids), 0, 0, ids[2], 1, 0, 0)),
                pl.BlockSpec(
                    (1, ny, nz, 1, 1, half, lanes), lambda i, ids: (at(i, ids), 0, 0, ids[2], 0, 0, width // lanes)
                ),
                pl.BlockSpec(wgu.shape, lambda i, ids: (0, 0), pipeline_mode=pl.Buffered(1)),
                pl.BlockSpec(wd.shape, lambda i, ids: (0, 0), pipeline_mode=pl.Buffered(1)),
            ],
            out_specs=[
                pl.BlockSpec((1, ny, nz, half, width), lambda i, ids: (i, 0, 0, 0, 0)),
                pl.BlockSpec((1, 2 * hid, count), lambda i, ids: (at(i, ids), 0, 0)),
                pl.BlockSpec((1, hid, count), lambda i, ids: (at(i, ids), 0, 0)),
            ],
        ),
        out_shape=[
            jax.ShapeDtypeStruct((nx, ny, nz, half, width), BF16),
            jax.ShapeDtypeStruct((nx, 2 * hid, count), BF16),
            jax.ShapeDtypeStruct((nx, hid, count), BF16),
        ],
        compiler_params=pltpu.CompilerParams(vmem_limit_bytes=56 << 20),
        name="tokens_first",
    )(ids, rows, rows, rows, wgu, wd)


def second_kernel(ids, *refs):
    t_parts, g_parts = refs[:5], refs[5:10]
    wgu_ref, wd_ref, p_ref, dgu_ref, h_ref, t_buf, g_buf, sems = refs[10:]
    step = pl.program_id(0)
    steps, half = t_buf.shape[1], t_buf.shape[1] // 2
    width = wgu_ref.shape[1]

    def copies(k):
        slot = k % 2
        if k == half:
            moves = [(t_parts[2], t_buf.at[slot, :half]), (t_parts[3], t_buf.at[slot, half:])]
        else:
            moves = [(t_parts[k if k < half else k + 1], t_buf.at[slot])]
        for y in range(steps):
            if y != half:
                source = g_parts[y if y < half else y + 1].at[k]
            elif k < half:
                source = g_parts[2].at[k]
            else:
                source = g_parts[3].at[k - half]
            moves.append((source, g_buf.at[slot, y]))
        return [pltpu.make_async_copy(a, b, sems.at[slot, n]) for n, (a, b) in enumerate(moves)]

    def run(k, method):
        for copy in copies(k):
            getattr(copy, method)()

    pl.when(step == 0)(lambda: run(0, "start"))
    for k in range(1, steps):
        pl.when(step == k - 1)(functools.partial(run, k, "start"))
    for k in range(steps):
        pl.when(step == k)(functools.partial(run, k, "wait"))
    slot = lax.rem(step, 2)
    rows = t_buf.shape[1] * t_buf.shape[2] * t_buf.shape[3]
    t = t_buf[slot, :, :, :, :width].reshape(rows, width)
    meta = t_buf[slot, :, :, :, width:].reshape(rows, -1)
    g = g_buf[slot].reshape(rows, width)
    expert_terms(ids, t, g, meta, wgu_ref, wd_ref, p_ref, dgu_ref, h_ref)


def second_call(ids, t_parts, g_parts, wgu, wd):
    ny, nz, half, wider = t_parts[0].shape
    nx, width = g_parts[0].shape[0], g_parts[0].shape[-1]
    hid = wd.shape[0]
    count = ny * nz * half
    hbm = pl.BlockSpec(memory_space=pl.ANY)
    return pl.pallas_call(
        second_kernel,
        grid_spec=pltpu.PrefetchScalarGridSpec(
            num_scalar_prefetch=1,
            grid=(nx,),
            in_specs=[hbm] * 10
            + [
                pl.BlockSpec(wgu.shape, lambda i, ids: (0, 0), pipeline_mode=pl.Buffered(1)),
                pl.BlockSpec(wd.shape, lambda i, ids: (0, 0), pipeline_mode=pl.Buffered(1)),
            ],
            out_specs=[
                pl.BlockSpec((ny, 1, nz, half, width), lambda i, ids: (0, i, 0, 0, 0)),
                pl.BlockSpec((1, 2 * hid, count), lambda i, ids: (i, 0, 0)),
                pl.BlockSpec((1, hid, count), lambda i, ids: (i, 0, 0)),
            ],
            scratch_shapes=[
                pltpu.VMEM((2, ny, nz, half, wider), BF16),
                pltpu.VMEM((2, ny, nz, half, width), BF16),
                pltpu.SemaphoreType.DMA((2, ny + 2)),
            ],
        ),
        out_shape=[
            jax.ShapeDtypeStruct((ny, nx, nz, half, width), BF16),
            jax.ShapeDtypeStruct((nx, 2 * hid, count), BF16),
            jax.ShapeDtypeStruct((nx, hid, count), BF16),
        ],
        compiler_params=pltpu.CompilerParams(vmem_limit_bytes=56 << 20),
        name="tokens_second",
    )(ids, *t_parts, *g_parts, wgu, wd)


def weight_kernel(ids, *refs):
    t_ref, g_ref = refs[:2]
    t_parts, g_parts = refs[2:7], refs[7:12]
    dgu0_ref, dgu1_ref, h0_ref, h1_ref, mine_ref, other_ref = refs[12:]
    nx, ny, nz, _, _, half, tile = t_ref.shape
    unit = h0_ref.shape[1] // 2
    flat = lambda a: a.reshape(-1, tile)

    def by_x(i):
        if i == nx // 2:
            return jnp.concatenate([flat(t_parts[2][...]), flat(t_parts[3][...])], axis=0)
        return flat(t_parts[i if i < nx // 2 else i + 1][...])

    def across(i):
        pieces = []
        for y in range(ny):
            if y != ny // 2:
                pieces.append(flat(g_parts[y if y < ny // 2 else y + 1][i]))
            else:
                pieces.append(flat(g_parts[2][i] if i < nx // 2 else g_parts[3][i - nx // 2]))
        return jnp.concatenate(pieces, axis=0)

    def outer(first, second, ref, right):
        total = None
        for i in range(nx):
            term = jnp.dot(first[i], flat(ref[i, :, :, 0, 0]), preferred_element_type=F32)
            total = term if total is None else total + term
        for i in range(nx):
            total = total + jnp.dot(second[i], right(i), preferred_element_type=F32)
        return total

    gu = outer(dgu0_ref, dgu1_ref, t_ref, by_x)
    down = outer(h0_ref, h1_ref, g_ref, across)
    mine_ref[0] = gu[:unit]
    mine_ref[1] = gu[2 * unit : 3 * unit]
    mine_ref[2] = down[:unit]
    other_ref[0] = gu[unit : 2 * unit].astype(BF16)
    other_ref[1] = gu[3 * unit :].astype(BF16)
    other_ref[2] = down[unit:].astype(BF16)


def weight_call(ids, rows, t_parts, g_parts, dgu0, dgu1, h0, h1):
    nx, ny, nz, _, _, half, _ = rows.shape
    width = g_parts[0].shape[-1]
    unit = h0.shape[1] // 2
    tile = 512
    whole = lambda a: pl.BlockSpec(a.shape, lambda j, ids: (0, 0, 0), pipeline_mode=pl.Buffered(1))
    part = lambda a: pl.BlockSpec((*a.shape[:3], tile), lambda j, ids: (0, 0, 0, j))
    return pl.pallas_call(
        weight_kernel,
        grid_spec=pltpu.PrefetchScalarGridSpec(
            num_scalar_prefetch=1,
            grid=(width // tile,),
            in_specs=[
                pl.BlockSpec((nx, ny, nz, 1, 1, half, tile), lambda j, ids: (0, 0, 0, ids[2], 0, 0, j)),
                pl.BlockSpec((nx, ny, nz, 1, 1, half, tile), lambda j, ids: (0, 0, 0, ids[2], 1, 0, j)),
                *(part(a) for a in t_parts),
                *(part(a) for a in g_parts),
                whole(dgu0),
                whole(dgu1),
                whole(h0),
                whole(h1),
            ],
            out_specs=[
                pl.BlockSpec((3, unit, tile), lambda j, ids: (0, 0, j)),
                pl.BlockSpec((3, unit, tile), lambda j, ids: (0, 0, j)),
            ],
        ),
        out_shape=[
            jax.ShapeDtypeStruct((3, unit, width), F32),
            jax.ShapeDtypeStruct((3, unit, width), BF16),
        ],
        compiler_params=pltpu.CompilerParams(vmem_limit_bytes=56 << 20),
        name="weights",
    )(ids, rows, rows, *t_parts, *g_parts, dgu0, dgu1, h0, h1)


def pick_weights(routes, router_weights, experts):
    hit = routes[:, :, None] == jnp.arange(experts, dtype=jnp.int32)[None, None, :]
    dense = jnp.sum(jnp.where(hit, router_weights[:, :, None], jnp.float32(0)), axis=1)
    high = lax.reduce_precision(dense, 8, 7)
    return jnp.concatenate([high, dense - high], axis=1).astype(BF16)


def on_device(tokens, out_grad, routes, router_weights, w_gate, w_up, w_down):
    nx, ny, nz, nc = (lax.axis_size(a) for a in ALL)
    ix, iy, iz, ic = (lax.axis_index(a) for a in ALL)
    per, width = tokens.shape
    half = per // 2
    experts = ny * nz * nc
    expert = (iy * nz + iz) * nc + ic
    ids = jnp.stack([ix, iy, ic, expert, expert + 1 - 2 * ic]).astype(jnp.int32)

    meta = pick_weights(routes, router_weights, experts)
    lanes = meta.shape[1]
    wider = jnp.concatenate([tokens, meta], axis=1)
    grads0 = jnp.concatenate([out_grad[:half], jnp.zeros((half, lanes), BF16)], axis=1)
    rows = lax.all_gather(jnp.concatenate([wider[:half], grads0], axis=0), ALL, axis=0, tiled=True)
    rows = rows.reshape(nx, ny, nz, nc, 2, half, width + lanes)

    t_z, g_z = ring_gather_z(wider[half:], out_grad[half:], "z")
    t_y, g_x, _ = ring_gather4(t_z, "y", g_z, "x")
    t_y, g_x = lax.optimization_barrier((joined4(t_y), joined4(g_x)))

    w_gate, w_up, w_down, _ = lax.optimization_barrier((w_gate, w_up, w_down, t_y))
    packed = jnp.concatenate([w_gate, w_up, w_down], axis=0)
    swapped = shift(packed, "c", 1)
    wgu = jnp.concatenate([w_gate[0], swapped[0], w_up[0], swapped[1]], axis=0)
    wd = jnp.concatenate([w_down[0], swapped[2]], axis=0)
    t_parts, g_parts, (wgu, wd) = ring_gather4(t_y, "x", g_x, "y", (wgu, wd))

    p1, dgu1, h1 = second_call(ids, t_parts, g_parts, wgu, wd)
    ends1 = ring_ends4(p1[2], "y")
    rows, dgu1 = lax.optimization_barrier((rows, dgu1))
    p0, dgu0, h0 = first_call(ids, rows, wgu, wd, lanes)
    ends1, p0, dgu0, h0 = lax.optimization_barrier((ends1, p0, dgu0, h0))
    ends0 = ring_ends4(p0[2], "x")
    near1, back1 = ring_middle4(p1[1], p1[3], ends1)
    last1 = ring_ends(near1, back1, "y")
    near0, back0 = ring_middle4(p0[1], p0[3], ends0)
    near0, back0, dgu0 = lax.optimization_barrier((near0, back0, dgu0))
    last0 = ring_ends(near0, back0, "x")
    mine, other = weight_call(ids, rows, t_parts, g_parts, dgu0, dgu1, h0, h1)
    last1, mine, other = lax.optimization_barrier((last1, mine, other))
    q1 = add(p1[0], *last1)
    r1 = ring_sum4(q1[0], q1[1], q1[2], q1[3], "x")
    r1 = lax.dynamic_slice_in_dim(jnp.concatenate([r1, r1], axis=0), nz - iz, nz, axis=0)
    q0 = add(p0[0], *last0)
    pick = lambda k: lax.dynamic_index_in_dim(q0, lax.rem(iy + k, ny), 0, keepdims=False)
    r0 = ring_sum4(pick(0), pick(1), pick(2), pick(3), "y")
    scatter = lambda r: lax.psum_scatter(r.reshape(nz * half, width), "z", scatter_dimension=0, tiled=True)
    grad_tokens = jnp.concatenate([scatter(r0), scatter(r1)], axis=0)

    grads = (mine + shift(other, "c", 1).astype(F32)).astype(BF16)
    return grad_tokens, grads[0:1], grads[1:2], grads[2:3]


def solution(mesh):
    fine = Mesh(mesh.devices.reshape(4, 4, 8, 2), ALL)
    row = P(ALL, None)
    weight = P(("y", "z", "c"), "x", None)
    return jax.shard_map(
        on_device,
        mesh=fine,
        in_specs=(row, row, row, row, weight, weight, weight),
        out_specs=(row, weight, weight, weight),
        check_vma=False,
    )
```

```python
import functools

import jax
import jax.numpy as jnp
from jax import lax
from jax.experimental import pallas as pl
from jax.experimental.pallas import tpu as pltpu
from jax.sharding import Mesh
from jax.sharding import PartitionSpec as P

BF16 = jnp.bfloat16
F32 = jnp.float32
ALL = ("x", "y", "z", "c")


def shift(value, axis, by):
    size = lax.axis_size(axis)
    return lax.ppermute(value, axis, [(i, (i + by) % size) for i in range(size)])


def add(first, *others):
    total = first.astype(F32)
    for other in others:
        total = total + other.astype(F32)
    return total.astype(BF16)


def ring_ends(up, down, axis):
    return shift(up, axis, 1), shift(down, axis, -1)


def ring_ends4(opposite, axis):
    half = opposite.shape[0] // 2
    return ring_ends(opposite[:half], opposite[half:], axis)


def ring_middle4(near, back, ends):
    half = ends[0].shape[0]
    near = jnp.concatenate([add(near[:half], ends[0]), near[half:]], axis=0)
    back = jnp.concatenate([back[:half], add(back[half:], ends[1])], axis=0)
    return near, back


def direct_sum(blocks, axis):
    size, far = len(blocks), len(blocks) // 2
    half = blocks[far].shape[0] // 2
    moved = [shift(b, axis, k if k < far else k - size) for k, b in enumerate(blocks) if k not in (0, far)]
    up, down = shift(blocks[far][:half], axis, far), shift(blocks[far][half:], axis, -far)
    total = blocks[0].astype(F32)
    for block in moved:
        total = total + block.astype(F32)
    return (total + jnp.concatenate([up, down], axis=0).astype(F32)).astype(BF16)


def ring_gather4(first, first_axis, second, second_axis, beside=()):
    near0, back0 = shift(first, first_axis, -1), shift(first, first_axis, 1)
    near1, back1 = shift(second, second_axis, -1), shift(second, second_axis, 1)
    near0, back0, near1, back1, beside = lax.optimization_barrier((near0, back0, near1, back1, beside))
    far = lambda near, back, axis, half: (shift(near[:half], axis, -1), shift(back[half:], axis, 1))
    far0 = far(near0, back0, first_axis, first.shape[0] // 2)
    far1 = far(near1, back1, second_axis, second.shape[0] // 2)
    return (first, near0, *far0, back0), (second, near1, *far1, back1), beside


def joined4(parts):
    own, near, first, second, back = parts
    return jnp.stack([own, near, jnp.concatenate([first, second], axis=0), back])


def ring_gather_z(left, right, axis):
    size, cut = lax.axis_size(axis), left.shape[1]
    own = jnp.concatenate([left, right], axis=1)
    up, down = [own], [own]
    for _ in range(size // 2 - 1):
        up.append(shift(up[-1], axis, -1))
        down.append(shift(down[-1], axis, 1))
    lefts = [b[:, :cut] for b in up] + [shift(up[-1][:, :cut], axis, -1)] + [b[:, :cut] for b in down[:0:-1]]
    rights = [b[:, cut:] for b in up] + [shift(down[-1][:, cut:], axis, 1)] + [b[:, cut:] for b in down[:0:-1]]
    return jnp.stack(lefts), jnp.stack(rights)


def expert_terms(ids, t, g, meta, wgu_ref, wd_ref, p_ref, dgu_ref, h_ref):
    rows, lanes = meta.shape
    hid = wd_ref.shape[0]
    lane = lax.rem(lax.broadcasted_iota(jnp.int32, (rows, lanes), 1), lanes // 2)
    values = meta.astype(F32)
    zero = jnp.float32(0)
    mine = jnp.sum(jnp.where(lane == ids[3], values, zero), axis=1, keepdims=True)
    other = jnp.sum(jnp.where(lane == ids[4], values, zero), axis=1, keepdims=True)
    column = lax.broadcasted_iota(jnp.int32, (rows, hid), 1)
    weight = jnp.where(column < hid // 2, mine, other)
    wide = (((1,), (1,)), ((), ()))
    gate_up = lax.dot_general(t, wgu_ref[...], wide, preferred_element_type=F32)
    back = lax.dot_general(g, wd_ref[...], wide, preferred_element_type=F32) * weight
    gate, upward = gate_up[:, :hid], gate_up[:, hid:]
    sigma = jax.nn.sigmoid(gate)
    active = gate * sigma
    hidden = (active * upward * weight).astype(BF16)
    d_gate = (back * upward * sigma * (1.0 + gate * (1.0 - sigma))).astype(BF16)
    d_up = (back * active).astype(BF16)
    both = jnp.concatenate([d_gate, d_up], axis=1)
    h_ref[...] = hidden.T.reshape(h_ref.shape)
    dgu_ref[...] = both.T.reshape(dgu_ref.shape)
    partial = jnp.dot(both, wgu_ref[...], preferred_element_type=F32)
    p_ref[...] = partial.astype(BF16).reshape(p_ref.shape)


def first_kernel(ids, t_ref, g_ref, m_ref, wgu_ref, wd_ref, p_ref, dgu_ref, h_ref):
    rows = t_ref.shape[1] * t_ref.shape[2] * t_ref.shape[5]
    flat = lambda ref: ref[...].reshape(rows, ref.shape[-1])
    expert_terms(ids, flat(t_ref), flat(g_ref), flat(m_ref), wgu_ref, wd_ref, p_ref, dgu_ref, h_ref)


def first_call(ids, rows, wgu, wd, lanes, start, stop, stride):
    nx, ny, nz, _, _, half, _ = rows.shape
    width = wgu.shape[1]
    hid = wd.shape[0]
    count = ny * nz * half
    steps = len(range(start, stop, stride))
    at = lambda i, ids: lax.rem(ids[0] + start + i * stride, nx)
    return pl.pallas_call(
        first_kernel,
        grid_spec=pltpu.PrefetchScalarGridSpec(
            num_scalar_prefetch=1,
            grid=(steps,),
            in_specs=[
                pl.BlockSpec((1, ny, nz, 1, 1, half, width), lambda i, ids: (at(i, ids), 0, 0, ids[2], 0, 0, 0)),
                pl.BlockSpec((1, ny, nz, 1, 1, half, width), lambda i, ids: (at(i, ids), 0, 0, ids[2], 1, 0, 0)),
                pl.BlockSpec(
                    (1, ny, nz, 1, 1, half, lanes), lambda i, ids: (at(i, ids), 0, 0, ids[2], 0, 0, width // lanes)
                ),
                pl.BlockSpec(wgu.shape, lambda i, ids: (0, 0), pipeline_mode=pl.Buffered(1)),
                pl.BlockSpec(wd.shape, lambda i, ids: (0, 0), pipeline_mode=pl.Buffered(1)),
            ],
            out_specs=[
                pl.BlockSpec((1, ny, nz, half, width), lambda i, ids: (i, 0, 0, 0, 0)),
                pl.BlockSpec((1, 2 * hid, count), lambda i, ids: (i, 0, 0)),
                pl.BlockSpec((1, hid, count), lambda i, ids: (i, 0, 0)),
            ],
        ),
        out_shape=[
            jax.ShapeDtypeStruct((steps, ny, nz, half, width), BF16),
            jax.ShapeDtypeStruct((steps, 2 * hid, count), BF16),
            jax.ShapeDtypeStruct((steps, hid, count), BF16),
        ],
        compiler_params=pltpu.CompilerParams(vmem_limit_bytes=56 << 20),
        name=f"tokens_first{start}",
    )(ids, rows, rows, rows, wgu, wd)


def second_kernel(ids, *refs):
    t_parts, g_parts = refs[:5], refs[5:10]
    wgu_ref, wd_ref, p_ref, dgu_ref, h_ref, t_buf, g_buf, sems = refs[10:]
    step = pl.program_id(0)
    steps, half = t_buf.shape[1], t_buf.shape[1] // 2
    width = wgu_ref.shape[1]

    def copies(k):
        slot = k % 2
        if k == half:
            moves = [(t_parts[2], t_buf.at[slot, :half]), (t_parts[3], t_buf.at[slot, half:])]
        else:
            moves = [(t_parts[k if k < half else k + 1], t_buf.at[slot])]
        for y in range(steps):
            if y != half:
                source = g_parts[y if y < half else y + 1].at[k]
            elif k < half:
                source = g_parts[2].at[k]
            else:
                source = g_parts[3].at[k - half]
            moves.append((source, g_buf.at[slot, y]))
        return [pltpu.make_async_copy(a, b, sems.at[slot, n]) for n, (a, b) in enumerate(moves)]

    def run(k, method):
        for copy in copies(k):
            getattr(copy, method)()

    pl.when(step == 0)(lambda: run(0, "start"))
    for k in range(1, steps):
        pl.when(step == k - 1)(functools.partial(run, k, "start"))
    for k in range(steps):
        pl.when(step == k)(functools.partial(run, k, "wait"))
    slot = lax.rem(step, 2)
    rows = t_buf.shape[1] * t_buf.shape[2] * t_buf.shape[3]
    t = t_buf[slot, :, :, :, :width].reshape(rows, width)
    meta = t_buf[slot, :, :, :, width:].reshape(rows, -1)
    g = g_buf[slot].reshape(rows, width)
    expert_terms(ids, t, g, meta, wgu_ref, wd_ref, p_ref, dgu_ref, h_ref)


def second_call(ids, t_parts, g_parts, wgu, wd):
    ny, nz, half, wider = t_parts[0].shape
    nx, width = g_parts[0].shape[0], g_parts[0].shape[-1]
    hid = wd.shape[0]
    count = ny * nz * half
    hbm = pl.BlockSpec(memory_space=pl.ANY)
    return pl.pallas_call(
        second_kernel,
        grid_spec=pltpu.PrefetchScalarGridSpec(
            num_scalar_prefetch=1,
            grid=(nx,),
            in_specs=[hbm] * 10
            + [
                pl.BlockSpec(wgu.shape, lambda i, ids: (0, 0), pipeline_mode=pl.Buffered(1)),
                pl.BlockSpec(wd.shape, lambda i, ids: (0, 0), pipeline_mode=pl.Buffered(1)),
            ],
            out_specs=[
                pl.BlockSpec((ny, 1, nz, half, width), lambda i, ids: (0, i, 0, 0, 0)),
                pl.BlockSpec((1, 2 * hid, count), lambda i, ids: (i, 0, 0)),
                pl.BlockSpec((1, hid, count), lambda i, ids: (i, 0, 0)),
            ],
            scratch_shapes=[
                pltpu.VMEM((2, ny, nz, half, wider), BF16),
                pltpu.VMEM((2, ny, nz, half, width), BF16),
                pltpu.SemaphoreType.DMA((2, ny + 2)),
            ],
        ),
        out_shape=[
            jax.ShapeDtypeStruct((ny, nx, nz, half, width), BF16),
            jax.ShapeDtypeStruct((nx, 2 * hid, count), BF16),
            jax.ShapeDtypeStruct((nx, hid, count), BF16),
        ],
        compiler_params=pltpu.CompilerParams(vmem_limit_bytes=56 << 20),
        name="tokens_second",
    )(ids, *t_parts, *g_parts, wgu, wd)


def weight_kernel(ids, *refs):
    t_ref, g_ref = refs[:2]
    t_parts, g_parts = refs[2:7], refs[7:12]
    dgu0_refs, h0_refs = refs[12:15], refs[15:18]
    dgu1_ref, h1_ref, mine_ref, other_ref = refs[18:]
    nx, ny, nz, _, _, half, tile = t_ref.shape
    unit = h1_ref.shape[1] // 2
    flat = lambda a: a.reshape(-1, tile)

    def by_x(i):
        if i == nx // 2:
            return jnp.concatenate([flat(t_parts[2][...]), flat(t_parts[3][...])], axis=0)
        return flat(t_parts[i if i < nx // 2 else i + 1][...])

    def across(i):
        pieces = []
        for y in range(ny):
            if y != ny // 2:
                pieces.append(flat(g_parts[y if y < ny // 2 else y + 1][i]))
            else:
                pieces.append(flat(g_parts[2][i] if i < nx // 2 else g_parts[3][i - nx // 2]))
        return jnp.concatenate(pieces, axis=0)

    def outer(first, second, ref, later):
        total = None
        blocks = first[0][0], first[1][0], first[2][0], first[1][1]
        for i in range(nx):
            right = flat(ref[lax.rem(ids[0] + i, nx), :, :, 0, 0])
            term = jnp.dot(blocks[i], right, preferred_element_type=F32)
            total = term if total is None else total + term
        for i in range(nx):
            total = total + jnp.dot(second[i], later(i), preferred_element_type=F32)
        return total

    gu = outer(dgu0_refs, dgu1_ref, t_ref, by_x)
    down = outer(h0_refs, h1_ref, g_ref, across)
    mine_ref[0] = gu[:unit]
    mine_ref[1] = gu[2 * unit : 3 * unit]
    mine_ref[2] = down[:unit]
    other_ref[0] = gu[unit : 2 * unit].astype(BF16)
    other_ref[1] = gu[3 * unit :].astype(BF16)
    other_ref[2] = down[unit:].astype(BF16)


def weight_call(ids, rows, t_parts, g_parts, dgu0, dgu1, h0, h1):
    nx, ny, nz, _, _, half, _ = rows.shape
    width = g_parts[0].shape[-1]
    unit = h1.shape[1] // 2
    tile = 512
    whole = lambda a: pl.BlockSpec(a.shape, lambda j, ids: (0, 0, 0), pipeline_mode=pl.Buffered(1))
    part = lambda a: pl.BlockSpec((*a.shape[:3], tile), lambda j, ids: (0, 0, 0, j))
    return pl.pallas_call(
        weight_kernel,
        grid_spec=pltpu.PrefetchScalarGridSpec(
            num_scalar_prefetch=1,
            grid=(width // tile,),
            in_specs=[
                pl.BlockSpec((nx, ny, nz, 1, 1, half, tile), lambda j, ids: (0, 0, 0, ids[2], 0, 0, j)),
                pl.BlockSpec((nx, ny, nz, 1, 1, half, tile), lambda j, ids: (0, 0, 0, ids[2], 1, 0, j)),
                *(part(a) for a in t_parts),
                *(part(a) for a in g_parts),
                *(whole(a) for a in (*dgu0, *h0, dgu1, h1)),
            ],
            out_specs=[
                pl.BlockSpec((3, unit, tile), lambda j, ids: (0, 0, j)),
                pl.BlockSpec((3, unit, tile), lambda j, ids: (0, 0, j)),
            ],
        ),
        out_shape=[
            jax.ShapeDtypeStruct((3, unit, width), F32),
            jax.ShapeDtypeStruct((3, unit, width), BF16),
        ],
        compiler_params=pltpu.CompilerParams(vmem_limit_bytes=56 << 20),
        name="weights",
    )(ids, rows, rows, *t_parts, *g_parts, *dgu0, *h0, dgu1, h1)


def pick_weights(routes, router_weights, experts):
    hit = routes[:, :, None] == jnp.arange(experts, dtype=jnp.int32)[None, None, :]
    dense = jnp.sum(jnp.where(hit, router_weights[:, :, None], jnp.float32(0)), axis=1)
    high = lax.reduce_precision(dense, 8, 7)
    return jnp.concatenate([high, dense - high], axis=1).astype(BF16)


def on_device(tokens, out_grad, routes, router_weights, w_gate, w_up, w_down):
    nx, ny, nz, nc = (lax.axis_size(a) for a in ALL)
    ix, iy, iz, ic = (lax.axis_index(a) for a in ALL)
    per, width = tokens.shape
    half = per // 2
    experts = ny * nz * nc
    expert = (iy * nz + iz) * nc + ic
    ids = jnp.stack([ix, iy, ic, expert, expert + 1 - 2 * ic]).astype(jnp.int32)

    meta = pick_weights(routes, router_weights, experts)
    lanes = meta.shape[1]
    wider = jnp.concatenate([tokens, meta], axis=1)
    grads0 = jnp.concatenate([out_grad[:half], jnp.zeros((half, lanes), BF16)], axis=1)
    rows = lax.all_gather(jnp.concatenate([wider[:half], grads0], axis=0), ALL, axis=0, tiled=True)
    rows = rows.reshape(nx, ny, nz, nc, 2, half, width + lanes)

    t_z, g_z = ring_gather_z(wider[half:], out_grad[half:], "z")
    t_y, g_x, _ = ring_gather4(t_z, "y", g_z, "x")
    t_y, g_x = lax.optimization_barrier((joined4(t_y), joined4(g_x)))

    w_gate, w_up, w_down, _ = lax.optimization_barrier((w_gate, w_up, w_down, t_y))
    packed = jnp.concatenate([w_gate, w_up, w_down], axis=0)
    swapped = shift(packed, "c", 1)
    wgu = jnp.concatenate([w_gate[0], swapped[0], w_up[0], swapped[1]], axis=0)
    wd = jnp.concatenate([w_down[0], swapped[2]], axis=0)
    t_parts, g_parts, (wgu, wd) = ring_gather4(t_y, "x", g_x, "y", (wgu, wd))

    p1, dgu1, h1 = second_call(ids, t_parts, g_parts, wgu, wd)
    ends1 = ring_ends4(p1[2], "y")
    rows, dgu1 = lax.optimization_barrier((rows, dgu1))
    first = functools.partial(first_call, ids, wgu=wgu, wd=wd, lanes=lanes)
    p_far, dgu_far, h_far = first(rows, start=2, stop=3, stride=1)
    ends1, p_far, rows = lax.optimization_barrier((ends1, p_far, rows))
    ends0 = ring_ends4(p_far[0], "x")
    last1 = ring_ends(*ring_middle4(p1[1], p1[3], ends1), "y")
    p_side, dgu_side, h_side = first(rows, start=1, stop=4, stride=2)
    ends0, p_side, rows = lax.optimization_barrier((ends0, p_side, rows))
    near0, back0 = ring_middle4(p_side[0], p_side[1], ends0)
    last0 = ring_ends(near0, back0, "x")
    near0, rows = lax.optimization_barrier((near0, rows))
    p_own, dgu_own, h_own = first(rows, start=0, stop=1, stride=1)
    mine, other = weight_call(
        ids, rows, t_parts, g_parts, (dgu_own, dgu_side, dgu_far), dgu1, (h_own, h_side, h_far), h1
    )
    last1, other = lax.optimization_barrier((last1, other))
    last0, mine = lax.optimization_barrier((last0, mine))
    grads = (mine + shift(other, "c", 1).astype(F32)).astype(BF16)
    q1 = add(p1[0], *last1)
    r1 = direct_sum([q1[k] for k in range(nx)], "x")
    r1 = lax.dynamic_slice_in_dim(jnp.concatenate([r1, r1], axis=0), nz - iz, nz, axis=0)
    q0 = add(p_own[0], *last0)
    r0 = direct_sum([lax.dynamic_index_in_dim(q0, lax.rem(iy + k, ny), 0, keepdims=False) for k in range(ny)], "y")
    both = jnp.concatenate([r0, r1], axis=1).reshape(nz * per, width)
    grad_tokens = lax.psum_scatter(both, "z", scatter_dimension=0, tiled=True)
    return grad_tokens, grads[0:1], grads[1:2], grads[2:3]


def solution(mesh):
    fine = Mesh(mesh.devices.reshape(4, 4, 8, 2), ALL)
    row = P(ALL, None)
    weight = P(("y", "z", "c"), "x", None)
    return jax.shard_map(
        on_device,
        mesh=fine,
        in_specs=(row, row, row, row, weight, weight, weight),
        out_specs=(row, weight, weight, weight),
        check_vma=False,
    )
```

```python
import functools

import jax
import jax.numpy as jnp
from jax import lax
from jax.experimental import pallas as pl
from jax.experimental.pallas import tpu as pltpu
from jax.sharding import Mesh
from jax.sharding import PartitionSpec as P

BF16 = jnp.bfloat16
F32 = jnp.float32
ALL = ("x", "y", "z", "c")


def shift(value, axis, by):
    size = lax.axis_size(axis)
    return lax.ppermute(value, axis, [(i, (i + by) % size) for i in range(size)])


def add(first, *others):
    total = first.astype(F32)
    for other in others:
        total = total + other.astype(F32)
    return total.astype(BF16)


def ring_ends(up, down, axis):
    return shift(up, axis, 1), shift(down, axis, -1)


def ring_ends4(opposite, axis):
    half = opposite.shape[0] // 2
    return ring_ends(opposite[:half], opposite[half:], axis)


def ring_middle4(near, back, ends):
    half = ends[0].shape[0]
    near = jnp.concatenate([add(near[:half], ends[0]), near[half:]], axis=0)
    back = jnp.concatenate([back[:half], add(back[half:], ends[1])], axis=0)
    return near, back


def direct_moves(blocks, axis, whole=False):
    size, far = len(blocks), len(blocks) // 2
    moved = [shift(b, axis, k if k < far else k - size) for k, b in enumerate(blocks) if k not in (0, far)]
    if whole:
        return moved + [shift(blocks[far], axis, far)]
    half = blocks[far].shape[0] // 2
    return moved, (shift(blocks[far][:half], axis, far), shift(blocks[far][half:], axis, -far))


def direct_total(own, moves):
    moved, halves = moves
    total = own.astype(F32)
    for block in moved:
        total = total + block.astype(F32)
    return (total + jnp.concatenate(halves, axis=0).astype(F32)).astype(BF16)


def ring_gather4(first, first_axis, second, second_axis, beside=()):
    near0, back0 = shift(first, first_axis, -1), shift(first, first_axis, 1)
    near1, back1 = shift(second, second_axis, -1), shift(second, second_axis, 1)
    near0, back0, near1, back1, beside = lax.optimization_barrier((near0, back0, near1, back1, beside))
    far = lambda near, back, axis, half: (shift(near[:half], axis, -1), shift(back[half:], axis, 1))
    far0 = far(near0, back0, first_axis, first.shape[0] // 2)
    far1 = far(near1, back1, second_axis, second.shape[0] // 2)
    return (first, near0, *far0, back0), (second, near1, *far1, back1), beside


def joined4(parts):
    own, near, first, second, back = parts
    return jnp.stack([own, near, jnp.concatenate([first, second], axis=0), back])


def ring_gather_z(left, right, axis):
    size, cut = lax.axis_size(axis), left.shape[1]
    own = jnp.concatenate([left, right], axis=1)
    up, down = [own], [own]
    for _ in range(size // 2 - 1):
        up.append(shift(up[-1], axis, -1))
        down.append(shift(down[-1], axis, 1))
    lefts = [b[:, :cut] for b in up] + [shift(up[-1][:, :cut], axis, -1)] + [b[:, :cut] for b in down[:0:-1]]
    rights = [b[:, cut:] for b in up] + [shift(down[-1][:, cut:], axis, 1)] + [b[:, cut:] for b in down[:0:-1]]
    return jnp.stack(lefts), jnp.stack(rights)


def expert_terms(ids, t, g, meta, wgu_ref, wd_ref, p_ref, dgu_ref, h_ref):
    rows, lanes = meta.shape
    hid = wd_ref.shape[0]
    lane = lax.rem(lax.broadcasted_iota(jnp.int32, (rows, lanes), 1), lanes // 2)
    values = meta.astype(F32)
    zero = jnp.float32(0)
    mine = jnp.sum(jnp.where(lane == ids[3], values, zero), axis=1, keepdims=True)
    other = jnp.sum(jnp.where(lane == ids[4], values, zero), axis=1, keepdims=True)
    column = lax.broadcasted_iota(jnp.int32, (rows, hid), 1)
    weight = jnp.where(column < hid // 2, mine, other)
    wide = (((1,), (1,)), ((), ()))
    gate_up = lax.dot_general(t, wgu_ref[...], wide, preferred_element_type=F32)
    back = lax.dot_general(g, wd_ref[...], wide, preferred_element_type=F32) * weight
    gate, upward = gate_up[:, :hid], gate_up[:, hid:]
    sigma = jax.nn.sigmoid(gate)
    active = gate * sigma
    hidden = (active * upward * weight).astype(BF16)
    d_gate = (back * upward * sigma * (1.0 + gate * (1.0 - sigma))).astype(BF16)
    d_up = (back * active).astype(BF16)
    both = jnp.concatenate([d_gate, d_up], axis=1)
    h_ref[...] = hidden.T.reshape(h_ref.shape)
    dgu_ref[...] = both.T.reshape(dgu_ref.shape)
    partial = jnp.dot(both, wgu_ref[...], preferred_element_type=F32)
    p_ref[...] = partial.astype(BF16).reshape(p_ref.shape)


def first_kernel(ids, t_ref, g_ref, m_ref, wgu_ref, wd_ref, p_ref, dgu_ref, h_ref):
    rows = t_ref.shape[1] * t_ref.shape[2] * t_ref.shape[5]
    flat = lambda ref: ref[...].reshape(rows, ref.shape[-1])
    expert_terms(ids, flat(t_ref), flat(g_ref), flat(m_ref), wgu_ref, wd_ref, p_ref, dgu_ref, h_ref)


def first_call(ids, rows, wgu, wd, lanes, start, stop, stride):
    nx, ny, nz, _, _, half, _ = rows.shape
    width = wgu.shape[1]
    hid = wd.shape[0]
    count = ny * nz * half
    steps = len(range(start, stop, stride))
    at = lambda i, ids: lax.rem(ids[0] + start + i * stride, nx)
    return pl.pallas_call(
        first_kernel,
        grid_spec=pltpu.PrefetchScalarGridSpec(
            num_scalar_prefetch=1,
            grid=(steps,),
            in_specs=[
                pl.BlockSpec((1, ny, nz, 1, 1, half, width), lambda i, ids: (at(i, ids), 0, 0, ids[2], 0, 0, 0)),
                pl.BlockSpec((1, ny, nz, 1, 1, half, width), lambda i, ids: (at(i, ids), 0, 0, ids[2], 1, 0, 0)),
                pl.BlockSpec(
                    (1, ny, nz, 1, 1, half, lanes), lambda i, ids: (at(i, ids), 0, 0, ids[2], 0, 0, width // lanes)
                ),
                pl.BlockSpec(wgu.shape, lambda i, ids: (0, 0), pipeline_mode=pl.Buffered(1)),
                pl.BlockSpec(wd.shape, lambda i, ids: (0, 0), pipeline_mode=pl.Buffered(1)),
            ],
            out_specs=[
                pl.BlockSpec((1, ny, nz, half, width), lambda i, ids: (i, 0, 0, 0, 0)),
                pl.BlockSpec((1, 2 * hid, count), lambda i, ids: (i, 0, 0)),
                pl.BlockSpec((1, hid, count), lambda i, ids: (i, 0, 0)),
            ],
        ),
        out_shape=[
            jax.ShapeDtypeStruct((steps, ny, nz, half, width), BF16),
            jax.ShapeDtypeStruct((steps, 2 * hid, count), BF16),
            jax.ShapeDtypeStruct((steps, hid, count), BF16),
        ],
        compiler_params=pltpu.CompilerParams(vmem_limit_bytes=56 << 20),
        name=f"tokens_first{start}",
    )(ids, rows, rows, rows, wgu, wd)


def second_kernel(ids, *refs):
    t_parts, g_parts = refs[:5], refs[5:10]
    wgu_ref, wd_ref, p_ref, dgu_ref, h_ref, t_buf, g_buf, sems = refs[10:]
    step = pl.program_id(0)
    steps, half = t_buf.shape[1], t_buf.shape[1] // 2
    width = wgu_ref.shape[1]

    def copies(k):
        slot = k % 2
        if k == half:
            moves = [(t_parts[2], t_buf.at[slot, :half]), (t_parts[3], t_buf.at[slot, half:])]
        else:
            moves = [(t_parts[k if k < half else k + 1], t_buf.at[slot])]
        for y in range(steps):
            if y != half:
                source = g_parts[y if y < half else y + 1].at[k]
            elif k < half:
                source = g_parts[2].at[k]
            else:
                source = g_parts[3].at[k - half]
            moves.append((source, g_buf.at[slot, y]))
        return [pltpu.make_async_copy(a, b, sems.at[slot, n]) for n, (a, b) in enumerate(moves)]

    def run(k, method):
        for copy in copies(k):
            getattr(copy, method)()

    pl.when(step == 0)(lambda: run(0, "start"))
    for k in range(1, steps):
        pl.when(step == k - 1)(functools.partial(run, k, "start"))
    for k in range(steps):
        pl.when(step == k)(functools.partial(run, k, "wait"))
    slot = lax.rem(step, 2)
    rows = t_buf.shape[1] * t_buf.shape[2] * t_buf.shape[3]
    t = t_buf[slot, :, :, :, :width].reshape(rows, width)
    meta = t_buf[slot, :, :, :, width:].reshape(rows, -1)
    g = g_buf[slot].reshape(rows, width)
    expert_terms(ids, t, g, meta, wgu_ref, wd_ref, p_ref, dgu_ref, h_ref)


def second_call(ids, t_parts, g_parts, wgu, wd):
    ny, nz, half, wider = t_parts[0].shape
    nx, width = g_parts[0].shape[0], g_parts[0].shape[-1]
    hid = wd.shape[0]
    count = ny * nz * half
    hbm = pl.BlockSpec(memory_space=pl.ANY)
    return pl.pallas_call(
        second_kernel,
        grid_spec=pltpu.PrefetchScalarGridSpec(
            num_scalar_prefetch=1,
            grid=(nx,),
            in_specs=[hbm] * 10
            + [
                pl.BlockSpec(wgu.shape, lambda i, ids: (0, 0), pipeline_mode=pl.Buffered(1)),
                pl.BlockSpec(wd.shape, lambda i, ids: (0, 0), pipeline_mode=pl.Buffered(1)),
            ],
            out_specs=[
                pl.BlockSpec((ny, 1, nz, half, width), lambda i, ids: (0, i, 0, 0, 0)),
                pl.BlockSpec((1, 2 * hid, count), lambda i, ids: (i, 0, 0)),
                pl.BlockSpec((1, hid, count), lambda i, ids: (i, 0, 0)),
            ],
            scratch_shapes=[
                pltpu.VMEM((2, ny, nz, half, wider), BF16),
                pltpu.VMEM((2, ny, nz, half, width), BF16),
                pltpu.SemaphoreType.DMA((2, ny + 2)),
            ],
        ),
        out_shape=[
            jax.ShapeDtypeStruct((ny, nx, nz, half, width), BF16),
            jax.ShapeDtypeStruct((nx, 2 * hid, count), BF16),
            jax.ShapeDtypeStruct((nx, hid, count), BF16),
        ],
        compiler_params=pltpu.CompilerParams(vmem_limit_bytes=56 << 20),
        name="tokens_second",
    )(ids, *t_parts, *g_parts, wgu, wd)


def weight_kernel(ids, *refs):
    t_ref, g_ref = refs[:2]
    t_parts, g_parts = refs[2:7], refs[7:12]
    dgu0_refs, h0_refs = refs[12:15], refs[15:18]
    dgu1_ref, h1_ref, mine_ref, other_ref = refs[18:]
    nx, ny, nz, _, _, half, tile = t_ref.shape
    unit = h1_ref.shape[1] // 2
    flat = lambda a: a.reshape(-1, tile)

    def by_x(i):
        if i == nx // 2:
            return jnp.concatenate([flat(t_parts[2][...]), flat(t_parts[3][...])], axis=0)
        return flat(t_parts[i if i < nx // 2 else i + 1][...])

    def across(i):
        pieces = []
        for y in range(ny):
            if y != ny // 2:
                pieces.append(flat(g_parts[y if y < ny // 2 else y + 1][i]))
            else:
                pieces.append(flat(g_parts[2][i] if i < nx // 2 else g_parts[3][i - nx // 2]))
        return jnp.concatenate(pieces, axis=0)

    def outer(first, second, ref, later):
        total = None
        blocks = first[0][0], first[1][0], first[2][0], first[1][1]
        for i in range(nx):
            right = flat(ref[lax.rem(ids[0] + i, nx), :, :, 0, 0])
            term = jnp.dot(blocks[i], right, preferred_element_type=F32)
            total = term if total is None else total + term
        for i in range(nx):
            total = total + jnp.dot(second[i], later(i), preferred_element_type=F32)
        return total

    gu = outer(dgu0_refs, dgu1_ref, t_ref, by_x)
    down = outer(h0_refs, h1_ref, g_ref, across)
    mine_ref[0] = gu[:unit]
    mine_ref[1] = gu[2 * unit : 3 * unit]
    mine_ref[2] = down[:unit]
    other_ref[0] = gu[unit : 2 * unit].astype(BF16)
    other_ref[1] = gu[3 * unit :].astype(BF16)
    other_ref[2] = down[unit:].astype(BF16)


def weight_call(ids, rows, t_parts, g_parts, dgu0, dgu1, h0, h1):
    nx, ny, nz, _, _, half, _ = rows.shape
    width = g_parts[0].shape[-1]
    unit = h1.shape[1] // 2
    tile = 512
    whole = lambda a: pl.BlockSpec(a.shape, lambda j, ids: (0, 0, 0), pipeline_mode=pl.Buffered(1))
    part = lambda a: pl.BlockSpec((*a.shape[:3], tile), lambda j, ids: (0, 0, 0, j))
    return pl.pallas_call(
        weight_kernel,
        grid_spec=pltpu.PrefetchScalarGridSpec(
            num_scalar_prefetch=1,
            grid=(width // tile,),
            in_specs=[
                pl.BlockSpec((nx, ny, nz, 1, 1, half, tile), lambda j, ids: (0, 0, 0, ids[2], 0, 0, j)),
                pl.BlockSpec((nx, ny, nz, 1, 1, half, tile), lambda j, ids: (0, 0, 0, ids[2], 1, 0, j)),
                *(part(a) for a in t_parts),
                *(part(a) for a in g_parts),
                *(whole(a) for a in (*dgu0, *h0, dgu1, h1)),
            ],
            out_specs=[
                pl.BlockSpec((3, unit, tile), lambda j, ids: (0, 0, j)),
                pl.BlockSpec((3, unit, tile), lambda j, ids: (0, 0, j)),
            ],
        ),
        out_shape=[
            jax.ShapeDtypeStruct((3, unit, width), F32),
            jax.ShapeDtypeStruct((3, unit, width), BF16),
        ],
        compiler_params=pltpu.CompilerParams(vmem_limit_bytes=56 << 20),
        name="weights",
    )(ids, rows, rows, *t_parts, *g_parts, *dgu0, *h0, dgu1, h1)


def pick_weights(routes, router_weights, experts):
    hit = routes[:, :, None] == jnp.arange(experts, dtype=jnp.int32)[None, None, :]
    dense = jnp.sum(jnp.where(hit, router_weights[:, :, None], jnp.float32(0)), axis=1)
    high = lax.reduce_precision(dense, 8, 7)
    return jnp.concatenate([high, dense - high], axis=1).astype(BF16)


def on_device(tokens, out_grad, routes, router_weights, w_gate, w_up, w_down):
    nx, ny, nz, nc = (lax.axis_size(a) for a in ALL)
    ix, iy, iz, ic = (lax.axis_index(a) for a in ALL)
    per, width = tokens.shape
    half = per // 2
    experts = ny * nz * nc
    expert = (iy * nz + iz) * nc + ic
    ids = jnp.stack([ix, iy, ic, expert, expert + 1 - 2 * ic]).astype(jnp.int32)

    meta = pick_weights(routes, router_weights, experts)
    lanes = meta.shape[1]
    wider = jnp.concatenate([tokens, meta], axis=1)
    grads0 = jnp.concatenate([out_grad[:half], jnp.zeros((half, lanes), BF16)], axis=1)
    rows = lax.all_gather(jnp.concatenate([wider[:half], grads0], axis=0), ALL, axis=0, tiled=True)
    rows = rows.reshape(nx, ny, nz, nc, 2, half, width + lanes)

    t_z, g_z = ring_gather_z(wider[half:], out_grad[half:], "z")
    t_y, g_x, _ = ring_gather4(t_z, "y", g_z, "x")
    t_y, g_x = lax.optimization_barrier((joined4(t_y), joined4(g_x)))

    w_gate, w_up, w_down, _ = lax.optimization_barrier((w_gate, w_up, w_down, t_y))
    packed = jnp.concatenate([w_gate, w_up, w_down], axis=0)
    swapped = shift(packed, "c", 1)
    wgu = jnp.concatenate([w_gate[0], swapped[0], w_up[0], swapped[1]], axis=0)
    wd = jnp.concatenate([w_down[0], swapped[2]], axis=0)
    t_parts, g_parts, (wgu, wd) = ring_gather4(t_y, "x", g_x, "y", (wgu, wd))

    p1, dgu1, h1 = second_call(ids, t_parts, g_parts, wgu, wd)
    ends1 = ring_ends4(p1[2], "y")
    rows, dgu1 = lax.optimization_barrier((rows, dgu1))
    first = functools.partial(first_call, ids, wgu=wgu, wd=wd, lanes=lanes)
    p_far, dgu_far, h_far = first(rows, start=2, stop=3, stride=1)
    ends0 = ring_ends4(p_far[0], "x")
    rows, dgu_far = lax.optimization_barrier((rows, dgu_far))
    p_side, dgu_side, h_side = first(rows, start=1, stop=4, stride=2)
    ends0, ends1, p_side, rows = lax.optimization_barrier((ends0, ends1, p_side, rows))
    near0, back0 = ring_middle4(p_side[0], p_side[1], ends0)
    last0 = ring_ends(near0, back0, "x")
    ends1, _ = lax.optimization_barrier((ends1, near0))
    last1 = ring_ends(*ring_middle4(p1[1], p1[3], ends1), "y")
    near0, rows = lax.optimization_barrier((near0, rows))
    p_own, dgu_own, h_own = first(rows, start=0, stop=1, stride=1)
    mine, other = weight_call(
        ids, rows, t_parts, g_parts, (dgu_own, dgu_side, dgu_far), dgu1, (h_own, h_side, h_far), h1
    )
    last1, other = lax.optimization_barrier((last1, other))
    last0, mine = lax.optimization_barrier((last0, mine))
    q1 = add(p1[0], *last1)
    moves1 = direct_moves([q1[k] for k in range(nx)], "x")
    q0 = add(p_own[0], *last0)
    moves1, _ = lax.optimization_barrier((moves1, q0))
    turned = lambda value, start, size: [
        lax.dynamic_index_in_dim(value, lax.rem(start + k, size), 0, keepdims=False) for k in range(size)
    ]
    blocks0 = turned(q0, iy, ny)
    moves0 = direct_moves(blocks0, "y")
    r1 = direct_total(q1[0], moves1)
    r1 = lax.dynamic_slice_in_dim(jnp.concatenate([r1, r1], axis=0), nz - iz, nz, axis=0)
    s1 = lax.psum_scatter(r1.reshape(nz * half, width), "z", scatter_dimension=0, tiled=True)
    grads = (mine + shift(other, "c", 1).astype(F32)).astype(BF16)
    moves0, grads = lax.optimization_barrier((moves0, grads))
    blocks0 = turned(direct_total(blocks0[0], moves0), iz, nz)
    s0 = add(blocks0[0], *direct_moves(blocks0, "z", whole=True))
    grad_tokens = jnp.concatenate([s0, s1], axis=0)
    return grad_tokens, grads[0:1], grads[1:2], grads[2:3]


def solution(mesh):
    fine = Mesh(mesh.devices.reshape(4, 4, 8, 2), ALL)
    row = P(ALL, None)
    weight = P(("y", "z", "c"), "x", None)
    return jax.shard_map(
        on_device,
        mesh=fine,
        in_specs=(row, row, row, row, weight, weight, weight),
        out_specs=(row, weight, weight, weight),
        check_vma=False,
    )
```

```python
import functools

import jax
import jax.numpy as jnp
from jax import lax
from jax.experimental import pallas as pl
from jax.experimental.pallas import tpu as pltpu
from jax.sharding import Mesh
from jax.sharding import PartitionSpec as P

BF16 = jnp.bfloat16
F32 = jnp.float32
ALL = ("x", "y", "z", "c")


def shift(value, axis, by):
    size = lax.axis_size(axis)
    return lax.ppermute(value, axis, [(i, (i + by) % size) for i in range(size)])


def add(first, *others):
    total = first.astype(F32)
    for other in others:
        total = total + other.astype(F32)
    return total.astype(BF16)


def ring_ends(up, down, axis):
    return shift(up, axis, 1), shift(down, axis, -1)


def ring_ends4(opposite, axis):
    half = opposite.shape[0] // 2
    return ring_ends(opposite[:half], opposite[half:], axis)


def ring_middle4(near, back, ends):
    half = ends[0].shape[0]
    near = jnp.concatenate([add(near[:half], ends[0]), near[half:]], axis=0)
    back = jnp.concatenate([back[:half], add(back[half:], ends[1])], axis=0)
    return near, back


def direct_moves(blocks, axis, whole=False):
    size, far = len(blocks), len(blocks) // 2
    moved = [shift(b, axis, k if k < far else k - size) for k, b in enumerate(blocks) if k not in (0, far)]
    if whole:
        return moved + [shift(blocks[far], axis, far)]
    half = blocks[far].shape[0] // 2
    return moved, (shift(blocks[far][:half], axis, far), shift(blocks[far][half:], axis, -far))


def direct_total(own, moves):
    moved, halves = moves
    total = own.astype(F32)
    for block in moved:
        total = total + block.astype(F32)
    return (total + jnp.concatenate(halves, axis=0).astype(F32)).astype(BF16)


def ring_gather4(first, first_axis, second, second_axis, beside=()):
    near0, back0 = shift(first, first_axis, -1), shift(first, first_axis, 1)
    near1, back1 = shift(second, second_axis, -1), shift(second, second_axis, 1)
    near0, back0, near1, back1, beside = lax.optimization_barrier((near0, back0, near1, back1, beside))
    far = lambda near, back, axis, half: (shift(near[:half], axis, -1), shift(back[half:], axis, 1))
    far0 = far(near0, back0, first_axis, first.shape[0] // 2)
    far1 = far(near1, back1, second_axis, second.shape[0] // 2)
    return (first, near0, *far0, back0), (second, near1, *far1, back1), beside


def joined4(parts):
    own, near, first, second, back = parts
    return jnp.stack([own, near, jnp.concatenate([first, second], axis=0), back])


def ring_gather_z(left, right, axis):
    size, cut = lax.axis_size(axis), left.shape[1]
    own = jnp.concatenate([left, right], axis=1)
    up, down = [own], [own]
    for _ in range(size // 2 - 1):
        up.append(shift(up[-1], axis, -1))
        down.append(shift(down[-1], axis, 1))
    lefts = [b[:, :cut] for b in up] + [shift(up[-1][:, :cut], axis, -1)] + [b[:, :cut] for b in down[:0:-1]]
    rights = [b[:, cut:] for b in up] + [shift(down[-1][:, cut:], axis, 1)] + [b[:, cut:] for b in down[:0:-1]]
    return jnp.stack(lefts), jnp.stack(rights)


def expert_terms(ids, t, g, meta, wgu_ref, wd_ref, p_ref, dgu_ref, h_ref):
    rows, lanes = meta.shape
    hid = wd_ref.shape[0]
    lane = lax.rem(lax.broadcasted_iota(jnp.int32, (rows, lanes), 1), lanes // 2)
    values = meta.astype(F32)
    zero = jnp.float32(0)
    mine = jnp.sum(jnp.where(lane == ids[3], values, zero), axis=1, keepdims=True)
    other = jnp.sum(jnp.where(lane == ids[4], values, zero), axis=1, keepdims=True)
    column = lax.broadcasted_iota(jnp.int32, (rows, hid), 1)
    weight = jnp.where(column < hid // 2, mine, other)
    wide = (((1,), (1,)), ((), ()))
    gate_up = lax.dot_general(t, wgu_ref[...], wide, preferred_element_type=F32)
    back = lax.dot_general(g, wd_ref[...], wide, preferred_element_type=F32) * weight
    gate, upward = gate_up[:, :hid], gate_up[:, hid:]
    sigma = jax.nn.sigmoid(gate)
    active = gate * sigma
    hidden = (active * upward * weight).astype(BF16)
    d_gate = (back * upward * sigma * (1.0 + gate * (1.0 - sigma))).astype(BF16)
    d_up = (back * active).astype(BF16)
    both = jnp.concatenate([d_gate, d_up], axis=1)
    h_ref[...] = hidden.T.reshape(h_ref.shape)
    dgu_ref[...] = both.T.reshape(dgu_ref.shape)
    partial = jnp.dot(both, wgu_ref[...], preferred_element_type=F32)
    p_ref[...] = partial.astype(BF16).reshape(p_ref.shape)


def first_kernel(ids, t_ref, g_ref, m_ref, wgu_ref, wd_ref, p_ref, dgu_ref, h_ref):
    rows = t_ref.shape[1] * t_ref.shape[2] * t_ref.shape[5]
    flat = lambda ref: ref[...].reshape(rows, ref.shape[-1])
    expert_terms(ids, flat(t_ref), flat(g_ref), flat(m_ref), wgu_ref, wd_ref, p_ref, dgu_ref, h_ref)


def first_call(ids, rows, wgu, wd, lanes, start, stop, stride):
    nx, ny, nz, _, _, half, _ = rows.shape
    width = wgu.shape[1]
    hid = wd.shape[0]
    count = ny * nz * half
    steps = len(range(start, stop, stride))
    at = lambda i, ids: lax.rem(ids[0] + start + i * stride, nx)
    return pl.pallas_call(
        first_kernel,
        grid_spec=pltpu.PrefetchScalarGridSpec(
            num_scalar_prefetch=1,
            grid=(steps,),
            in_specs=[
                pl.BlockSpec((1, ny, nz, 1, 1, half, width), lambda i, ids: (at(i, ids), 0, 0, ids[2], 0, 0, 0)),
                pl.BlockSpec((1, ny, nz, 1, 1, half, width), lambda i, ids: (at(i, ids), 0, 0, ids[2], 1, 0, 0)),
                pl.BlockSpec(
                    (1, ny, nz, 1, 1, half, lanes), lambda i, ids: (at(i, ids), 0, 0, ids[2], 0, 0, width // lanes)
                ),
                pl.BlockSpec(wgu.shape, lambda i, ids: (0, 0), pipeline_mode=pl.Buffered(1)),
                pl.BlockSpec(wd.shape, lambda i, ids: (0, 0), pipeline_mode=pl.Buffered(1)),
            ],
            out_specs=[
                pl.BlockSpec((1, ny, nz, half, width), lambda i, ids: (i, 0, 0, 0, 0)),
                pl.BlockSpec((1, 2 * hid, count), lambda i, ids: (i, 0, 0)),
                pl.BlockSpec((1, hid, count), lambda i, ids: (i, 0, 0)),
            ],
        ),
        out_shape=[
            jax.ShapeDtypeStruct((steps, ny, nz, half, width), BF16),
            jax.ShapeDtypeStruct((steps, 2 * hid, count), BF16),
            jax.ShapeDtypeStruct((steps, hid, count), BF16),
        ],
        compiler_params=pltpu.CompilerParams(vmem_limit_bytes=56 << 20),
        name=f"tokens_first{start}",
    )(ids, rows, rows, rows, wgu, wd)


def second_kernel(ids, *refs):
    t_parts, g_parts = refs[:5], refs[5:10]
    wgu_ref, wd_ref, p_ref, dgu_ref, h_ref, t_buf, g_buf, sems = refs[10:]
    step = pl.program_id(0)
    steps, half = t_buf.shape[1], t_buf.shape[1] // 2
    width = wgu_ref.shape[1]

    def copies(k):
        slot = k % 2
        if k == half:
            moves = [(t_parts[2], t_buf.at[slot, :half]), (t_parts[3], t_buf.at[slot, half:])]
        else:
            moves = [(t_parts[k if k < half else k + 1], t_buf.at[slot])]
        for y in range(steps):
            if y != half:
                source = g_parts[y if y < half else y + 1].at[k]
            elif k < half:
                source = g_parts[2].at[k]
            else:
                source = g_parts[3].at[k - half]
            moves.append((source, g_buf.at[slot, y]))
        return [pltpu.make_async_copy(a, b, sems.at[slot, n]) for n, (a, b) in enumerate(moves)]

    def run(k, method):
        for copy in copies(k):
            getattr(copy, method)()

    pl.when(step == 0)(lambda: run(0, "start"))
    for k in range(1, steps):
        pl.when(step == k - 1)(functools.partial(run, k, "start"))
    for k in range(steps):
        pl.when(step == k)(functools.partial(run, k, "wait"))
    slot = lax.rem(step, 2)
    rows = t_buf.shape[1] * t_buf.shape[2] * t_buf.shape[3]
    t = t_buf[slot, :, :, :, :width].reshape(rows, width)
    meta = t_buf[slot, :, :, :, width:].reshape(rows, -1)
    g = g_buf[slot].reshape(rows, width)
    expert_terms(ids, t, g, meta, wgu_ref, wd_ref, p_ref, dgu_ref, h_ref)


def second_call(ids, t_parts, g_parts, wgu, wd):
    ny, nz, half, wider = t_parts[0].shape
    nx, width = g_parts[0].shape[0], g_parts[0].shape[-1]
    hid = wd.shape[0]
    count = ny * nz * half
    hbm = pl.BlockSpec(memory_space=pl.ANY)
    return pl.pallas_call(
        second_kernel,
        grid_spec=pltpu.PrefetchScalarGridSpec(
            num_scalar_prefetch=1,
            grid=(nx,),
            in_specs=[hbm] * 10
            + [
                pl.BlockSpec(wgu.shape, lambda i, ids: (0, 0), pipeline_mode=pl.Buffered(1)),
                pl.BlockSpec(wd.shape, lambda i, ids: (0, 0), pipeline_mode=pl.Buffered(1)),
            ],
            out_specs=[
                pl.BlockSpec((ny, 1, nz, half, width), lambda i, ids: (0, i, 0, 0, 0)),
                pl.BlockSpec((1, 2 * hid, count), lambda i, ids: (i, 0, 0)),
                pl.BlockSpec((1, hid, count), lambda i, ids: (i, 0, 0)),
            ],
            scratch_shapes=[
                pltpu.VMEM((2, ny, nz, half, wider), BF16),
                pltpu.VMEM((2, ny, nz, half, width), BF16),
                pltpu.SemaphoreType.DMA((2, ny + 2)),
            ],
        ),
        out_shape=[
            jax.ShapeDtypeStruct((ny, nx, nz, half, width), BF16),
            jax.ShapeDtypeStruct((nx, 2 * hid, count), BF16),
            jax.ShapeDtypeStruct((nx, hid, count), BF16),
        ],
        compiler_params=pltpu.CompilerParams(vmem_limit_bytes=56 << 20),
        name="tokens_second",
    )(ids, *t_parts, *g_parts, wgu, wd)


def weight_kernel(ids, *refs):
    t_ref, g_ref = refs[:2]
    t_parts, g_parts = refs[2:7], refs[7:12]
    dgu0_refs, h0_refs = refs[12:15], refs[15:18]
    dgu1_ref, h1_ref, mine_ref, other_ref = refs[18:]
    nx, ny, nz, _, _, half, tile = t_ref.shape
    unit = h1_ref.shape[1] // 2
    flat = lambda a: a.reshape(-1, tile)

    def by_x(i):
        if i == nx // 2:
            return jnp.concatenate([flat(t_parts[2][...]), flat(t_parts[3][...])], axis=0)
        return flat(t_parts[i if i < nx // 2 else i + 1][...])

    def across(i):
        pieces = []
        for y in range(ny):
            if y != ny // 2:
                pieces.append(flat(g_parts[y if y < ny // 2 else y + 1][i]))
            else:
                pieces.append(flat(g_parts[2][i] if i < nx // 2 else g_parts[3][i - nx // 2]))
        return jnp.concatenate(pieces, axis=0)

    def outer(first, second, ref, later):
        total = None
        blocks = first[0][0], first[1][0], first[2][0], first[1][1]
        for i in range(nx):
            right = flat(ref[lax.rem(ids[0] + i, nx), :, :, 0, 0])
            term = jnp.dot(blocks[i], right, preferred_element_type=F32)
            total = term if total is None else total + term
        for i in range(nx):
            total = total + jnp.dot(second[i], later(i), preferred_element_type=F32)
        return total

    gu = outer(dgu0_refs, dgu1_ref, t_ref, by_x)
    down = outer(h0_refs, h1_ref, g_ref, across)
    mine_ref[0] = gu[:unit]
    mine_ref[1] = gu[2 * unit : 3 * unit]
    mine_ref[2] = down[:unit]
    other_ref[0] = gu[unit : 2 * unit].astype(BF16)
    other_ref[1] = gu[3 * unit :].astype(BF16)
    other_ref[2] = down[unit:].astype(BF16)


def weight_call(ids, rows, t_parts, g_parts, dgu0, dgu1, h0, h1):
    nx, ny, nz, _, _, half, _ = rows.shape
    width = g_parts[0].shape[-1]
    unit = h1.shape[1] // 2
    tile = 512
    whole = lambda a: pl.BlockSpec(a.shape, lambda j, ids: (0, 0, 0), pipeline_mode=pl.Buffered(1))
    part = lambda a: pl.BlockSpec((*a.shape[:3], tile), lambda j, ids: (0, 0, 0, j))
    return pl.pallas_call(
        weight_kernel,
        grid_spec=pltpu.PrefetchScalarGridSpec(
            num_scalar_prefetch=1,
            grid=(width // tile,),
            in_specs=[
                pl.BlockSpec((nx, ny, nz, 1, 1, half, tile), lambda j, ids: (0, 0, 0, ids[2], 0, 0, j)),
                pl.BlockSpec((nx, ny, nz, 1, 1, half, tile), lambda j, ids: (0, 0, 0, ids[2], 1, 0, j)),
                *(part(a) for a in t_parts),
                *(part(a) for a in g_parts),
                *(whole(a) for a in (*dgu0, *h0, dgu1, h1)),
            ],
            out_specs=[
                pl.BlockSpec((3, unit, tile), lambda j, ids: (0, 0, j)),
                pl.BlockSpec((3, unit, tile), lambda j, ids: (0, 0, j)),
            ],
        ),
        out_shape=[
            jax.ShapeDtypeStruct((3, unit, width), F32),
            jax.ShapeDtypeStruct((3, unit, width), BF16),
        ],
        compiler_params=pltpu.CompilerParams(vmem_limit_bytes=56 << 20),
        name="weights",
    )(ids, rows, rows, *t_parts, *g_parts, *dgu0, *h0, dgu1, h1)


def pick_weights(routes, router_weights, experts):
    hit = routes[:, :, None] == jnp.arange(experts, dtype=jnp.int32)[None, None, :]
    dense = jnp.sum(jnp.where(hit, router_weights[:, :, None], jnp.float32(0)), axis=1)
    high = lax.reduce_precision(dense, 8, 7)
    return jnp.concatenate([high, dense - high], axis=1).astype(BF16)


def on_device(tokens, out_grad, routes, router_weights, w_gate, w_up, w_down):
    nx, ny, nz, nc = (lax.axis_size(a) for a in ALL)
    ix, iy, iz, ic = (lax.axis_index(a) for a in ALL)
    per, width = tokens.shape
    half = per // 2
    experts = ny * nz * nc
    expert = (iy * nz + iz) * nc + ic
    ids = jnp.stack([ix, iy, ic, expert, expert + 1 - 2 * ic]).astype(jnp.int32)

    meta = pick_weights(routes, router_weights, experts)
    lanes = meta.shape[1]
    wider = jnp.concatenate([tokens, meta], axis=1)
    grads0 = jnp.concatenate([out_grad[:half], jnp.zeros((half, lanes), BF16)], axis=1)
    rows = lax.all_gather(jnp.concatenate([wider[:half], grads0], axis=0), ALL, axis=0, tiled=True)
    rows = rows.reshape(nx, ny, nz, nc, 2, half, width + lanes)

    t_z, g_z = ring_gather_z(wider[half:], out_grad[half:], "z")
    t_y, g_x, _ = ring_gather4(t_z, "y", g_z, "x")
    t_y, g_x = lax.optimization_barrier((joined4(t_y), joined4(g_x)))

    w_gate, w_up, w_down, _ = lax.optimization_barrier((w_gate, w_up, w_down, t_y))
    packed = jnp.concatenate([w_gate, w_up, w_down], axis=0)
    swapped = shift(packed, "c", 1)
    wgu = jnp.concatenate([w_gate[0], swapped[0], w_up[0], swapped[1]], axis=0)
    wd = jnp.concatenate([w_down[0], swapped[2]], axis=0)
    t_parts, g_parts, (wgu, wd) = ring_gather4(t_y, "x", g_x, "y", (wgu, wd))

    p1, dgu1, h1 = second_call(ids, t_parts, g_parts, wgu, wd)
    ends1 = ring_ends4(p1[2], "y")
    rows, dgu1 = lax.optimization_barrier((rows, dgu1))
    first = functools.partial(first_call, ids, wgu=wgu, wd=wd, lanes=lanes)
    p_far, dgu_far, h_far = first(rows, start=2, stop=3, stride=1)
    ends0 = ring_ends4(p_far[0], "x")
    rows, dgu_far = lax.optimization_barrier((rows, dgu_far))
    p_side, dgu_side, h_side = first(rows, start=1, stop=4, stride=2)
    ends0, ends1, p_side, rows = lax.optimization_barrier((ends0, ends1, p_side, rows))
    near0, back0 = ring_middle4(p_side[0], p_side[1], ends0)
    last0 = ring_ends(near0, back0, "x")
    ends1, _ = lax.optimization_barrier((ends1, near0))
    last1 = ring_ends(*ring_middle4(p1[1], p1[3], ends1), "y")
    near0, rows = lax.optimization_barrier((near0, rows))
    p_own, dgu_own, h_own = first(rows, start=0, stop=1, stride=1)
    mine, other = weight_call(
        ids, rows, t_parts, g_parts, (dgu_own, dgu_side, dgu_far), dgu1, (h_own, h_side, h_far), h1
    )
    last1, other = lax.optimization_barrier((last1, other))
    last0, mine = lax.optimization_barrier((last0, mine))
    turned = lambda value, start, size: [
        lax.dynamic_index_in_dim(value, lax.rem(start + k, size), 0, keepdims=False) for k in range(size)
    ]
    q0 = add(p_own[0], *last0)
    blocks0 = turned(q0, iy, ny)
    moves0 = direct_moves(blocks0, "y")
    last1, _ = lax.optimization_barrier((last1, q0))
    q1 = add(p1[0], *last1)
    moves1 = direct_moves([q1[k] for k in range(nx)], "x")
    r0 = direct_total(blocks0[0], moves0)
    r1 = direct_total(q1[0], moves1)
    blocks = [jnp.concatenate([r, r1[k]], axis=0) for k, r in enumerate(turned(r0, iz, nz))]
    other, _ = lax.optimization_barrier((other, r1))
    grads = (mine + shift(other, "c", 1).astype(F32)).astype(BF16)
    moves, grads = lax.optimization_barrier((direct_moves(blocks, "z", whole=True), grads))
    grad_tokens = add(blocks[0], *moves)
    return grad_tokens, grads[0:1], grads[1:2], grads[2:3]


def solution(mesh):
    fine = Mesh(mesh.devices.reshape(4, 4, 8, 2), ALL)
    row = P(ALL, None)
    weight = P(("y", "z", "c"), "x", None)
    return jax.shard_map(
        on_device,
        mesh=fine,
        in_specs=(row, row, row, row, weight, weight, weight),
        out_specs=(row, weight, weight, weight),
        check_vma=False,
    )
```
